32 devices in a mesh: seg: 2 (over x), rows: 16 (over z, y, core).
Axes of the slice: x: 2, y: 2, z: 4, core: 2. Of those that a mesh axis runs over, the one named last changes fastest.
Arguments:
- snapshots: float32 [512, 131072], P('seg', 'rows'), parts along dimension 0, may hold values from -400 to 400
Outputs:
- q_panel: float32 [64, 131072], P('seg', 'rows'), parts along dimension 0
- r_panel: float32 [64, 32], P('seg'), parts along dimension 0
- projected: float32 [64, 224], P('seg'), parts along dimension 0
- trailing: float32 [448, 131072], P('seg', 'rows'), parts along dimension 0
The draws below stay inside these ranges and needn't reach their ends.
There are 2 independent parts, one for each index of `seg`. The reference program is written for one: setup_inputs(seed, part) draws one part's arguments, and reference() takes and returns one part's arrays. A program takes and returns all parts, laid end to end along the dimension named above; each array names one. Nothing has to cross between parts.
All inputs are finite; a program needn't handle non-finite values.
Results may differ from the reference program's by a relative error of at most 0.000082.
Values sent between devices are 32-bit elements; how exact they have to be, the bound alone decides.
A program may use at most 64 MiB of HBM per device.

```python
import jax
import jax.numpy as jnp
from jax import lax

COLS = 256
PANEL = 32
HEIGHT = 131072


def draw_snapshots(key, part):
    keys = jax.random.split(jax.random.fold_in(key, 17), 4)
    base = jax.random.normal(keys[0], (COLS, HEIGHT), jnp.float32)
    mixing = jax.random.normal(keys[1], (COLS - PANEL, PANEL), jnp.float32) * (1.5 / PANEL ** 0.5)
    lead = base[:PANEL]
    tail = 0.5 * base[PANEL:] + jnp.dot(mixing, lead, precision=lax.Precision.HIGHEST)
    whole = jnp.concatenate([lead, tail], axis=0)
    position = jnp.arange(HEIGHT, dtype=jnp.float32) / HEIGHT
    row_scale = jnp.exp(jax.random.uniform(keys[2], (1, HEIGHT)) * jnp.log(10.0)) * (1.0 + 2.0 * position)[None, :]
    col_scale = jnp.exp(jax.random.uniform(keys[3], (COLS, 1)) * jnp.log(10.0))
    return jnp.clip(whole * row_scale * col_scale * 0.25, -400.0, 400.0)


def setup_inputs(seed: int = 0, part: int = 0) -> dict:
    splits = jax.random.split(jax.random.key(seed), 2)
    part_keys = jax.random.split(jax.random.fold_in(splits[1], part), 2)
    snapshots = draw_snapshots(jax.random.fold_in(jax.random.fold_in(splits[1], part), 71), part)
    return dict(snapshots=snapshots)


def inner(left, right):
    return lax.dot_general(left.astype(jnp.float32), right.astype(jnp.float32), (((1,), (1,)), ((), ())), precision=lax.Precision.HIGHEST, preferred_element_type=jnp.float32)

def reference(snapshots):
    panel = snapshots[:PANEL]
    rest = snapshots[PANEL:]
    gram = inner(panel, panel)
    lower = jnp.linalg.cholesky(gram)
    q_panel = jax.scipy.linalg.solve_triangular(lower, panel, lower=True)
    projected = inner(q_panel, rest)
    update = lax.dot_general(projected.astype(jnp.float32), q_panel.astype(jnp.float32), (((0,), (0,)), ((), ())), precision=lax.Precision.HIGHEST, preferred_element_type=jnp.float32)
    trailing = rest - update
    return (q_panel, lower.T, projected, trailing)
```

```python
import functools

import jax
import jax.numpy as jnp
from jax import lax
from jax.experimental import pallas as pl
from jax.experimental.pallas import tpu as pltpu
from jax.sharding import PartitionSpec as P

PANEL = 32
CHUNK = 1024
MESH = pl.DeviceIdType.MESH


def split(value):
    high = value.astype(jnp.bfloat16)
    return high, (value - high.astype(jnp.float32)).astype(jnp.bfloat16)


def reduce_kernel(chips, x_hbm, snap, stack, total, acc, part, pair_in, slots, full,
                  load_sem, pair_send, pair_recv, chip_send, chip_recv, last_send, last_recv):
    me = lax.axis_index("rows")
    core = lax.rem(me, 2)
    chip = lax.div(me, 2)
    partner = me + 1 - 2 * core
    cols, width = snap.shape
    chunks = width // CHUNK

    def load(c):
        where = pl.ds(pl.multiple_of(c * CHUNK, CHUNK), CHUNK)
        return pltpu.make_async_copy(x_hbm.at[:, where], snap.at[:, where], load_sem.at[c])

    for c in range(chunks):
        load(c).start()

    barrier = pltpu.get_barrier_semaphore()
    pl.semaphore_signal(barrier, inc=1, device_id={"rows": partner}, device_id_type=MESH)
    for k in range(1, chips):
        peer = lax.rem(chip + k, chips) * 2 + core
        pl.semaphore_signal(barrier, inc=1, device_id={"rows": peer}, device_id_type=MESH)

    acc[...] = jnp.zeros_like(acc)
    for c in range(chunks):
        load(c).wait()
        where = pl.ds(c * CHUNK, CHUNK)
        high, low = split(snap[:, where])
        panel = jnp.concatenate([high[:PANEL], low[:PANEL]], axis=0)
        stack[:, where] = panel
        acc[...] += lax.dot_general(
            jnp.concatenate([high, low], axis=0), panel, (((1,), (1,)), ((), ())),
            preferred_element_type=jnp.float32)
    both = acc[:cols] + acc[cols:]
    gram = (both[:, :PANEL] + both[:, PANEL:]).T
    half = PANEL // 2
    part[0] = gram[:half]
    part[1] = gram[half:]

    pl.semaphore_wait(barrier, chips)
    pair = pltpu.make_async_remote_copy(
        src_ref=part.at[1 - core], dst_ref=pair_in, send_sem=pair_send, recv_sem=pair_recv,
        device_id={"rows": partner}, device_id_type=MESH)
    pair.start()
    pair.wait()
    slots[chip] = part[core] + pair_in[...]

    def send(k):
        peer = lax.rem(chip + k, chips) * 2 + core
        return pltpu.make_async_remote_copy(
            src_ref=slots.at[chip], dst_ref=slots.at[chip], send_sem=chip_send.at[k - 1],
            recv_sem=chip_recv.at[k - 1], device_id={"rows": peer}, device_id_type=MESH)

    for k in range(1, chips):
        send(k).start()
    for k in range(1, chips):
        send(k).wait_recv()
    whole = slots[0]
    for k in range(1, chips):
        whole = whole + slots[k]
    full[core] = whole
    last = pltpu.make_async_remote_copy(
        src_ref=full.at[core], dst_ref=full.at[core], send_sem=last_send, recv_sem=last_recv,
        device_id={"rows": partner}, device_id_type=MESH)
    last.start()
    for k in range(1, chips):
        send(k).wait_send()
    last.wait()
    total[...] = full[...]


def update_kernel(snap, stack, total, q_ref, r_ref, projected_ref, trailing_ref, coef):
    step = pl.program_id(0)
    cols = snap.shape[0]

    @pl.when(step == 0)
    def _():
        a = total[...].reshape(PANEL, cols)
        rows = lax.broadcasted_iota(jnp.int32, (PANEL, 1), 0)
        eye = jnp.where(rows == lax.broadcasted_iota(jnp.int32, (PANEL, PANEL), 1), 1.0, 0.0)
        inv = eye
        upper, lower = jnp.zeros_like(a), jnp.zeros_like(inv)
        pivots = jnp.zeros((PANEL, 1), jnp.float32)
        for j in range(PANEL):
            at = rows == j
            pivot = a[j:j + 1, j:j + 1]
            upper = jnp.where(at, a, upper)
            lower = jnp.where(at, inv, lower)
            pivots = jnp.where(at, pivot, pivots)
            column = a[:, j:j + 1]
            recip = 1.0 / pivot
            a_row, inv_row = a[j:j + 1] * recip, inv[j:j + 1] * recip
            a = jnp.where(at, a_row, a - column * a_row)
            inv = jnp.where(at, inv_row, inv - column * inv_row)
        scale = 1.0 / jnp.sqrt(pivots)
        upper, lower = upper * scale, lower * scale
        lanes = lax.broadcasted_iota(jnp.int32, (PANEL, PANEL), 1)
        r_ref[...] = jnp.where(lanes >= rows, upper[:, :PANEL], 0.0)
        projected_ref[...] = upper[:, PANEL:]
        lower = jnp.where(lanes <= rows, lower, 0.0)
        weights = jnp.concatenate([lower, -(a.T)[PANEL:]], axis=0)
        high, low = split(weights)
        coef[...] = jnp.concatenate([high, high, low, low], axis=1)

    where = pl.ds(pl.multiple_of(step * CHUNK, CHUNK), CHUNK)
    panel = stack[:, where]
    out = lax.dot_general(
        coef[...], jnp.concatenate([panel, panel], axis=0), (((1,), (0,)), ((), ())),
        preferred_element_type=jnp.float32)
    q_ref[...] = out[:PANEL]
    trailing_ref[...] = snap[PANEL:, where] + out[PANEL:]


def local(rows, snapshots):
    cols, width = snapshots.shape
    chips = rows // 2
    half = PANEL // 2
    f32 = jnp.float32
    vmem = pl.BlockSpec(memory_space=pltpu.VMEM)
    snap, stack, total = pl.pallas_call(
        functools.partial(reduce_kernel, chips),
        out_shape=(
            pltpu.VMEM((cols, width), f32),
            pltpu.VMEM((2 * PANEL, width), jnp.bfloat16),
            pltpu.VMEM((2, half, cols), f32)),
        in_specs=[pl.BlockSpec(memory_space=pltpu.HBM)],
        out_specs=(vmem, vmem, vmem),
        scratch_shapes=[
            pltpu.VMEM((2 * cols, 2 * PANEL), f32),
            pltpu.VMEM((2, half, cols), f32),
            pltpu.VMEM((half, cols), f32),
            pltpu.VMEM((chips, half, cols), f32),
            pltpu.VMEM((2, half, cols), f32),
            pltpu.SemaphoreType.DMA((width // CHUNK,)),
            pltpu.SemaphoreType.DMA,
            pltpu.SemaphoreType.DMA,
            pltpu.SemaphoreType.DMA((chips - 1,)),
            pltpu.SemaphoreType.DMA((chips - 1,)),
            pltpu.SemaphoreType.DMA,
            pltpu.SemaphoreType.DMA,
        ],
        compiler_params=pltpu.CompilerParams(
            collective_id=0, has_side_effects=True, vmem_limit_bytes=24 << 20),
        name="reduce",
    )(snapshots)
    return pl.pallas_call(
        update_kernel,
        grid=(width // CHUNK,),
        out_shape=(
            jax.ShapeDtypeStruct((PANEL, width), f32),
            jax.ShapeDtypeStruct((PANEL, PANEL), f32),
            jax.ShapeDtypeStruct((PANEL, cols - PANEL), f32),
            jax.ShapeDtypeStruct((cols - PANEL, width), f32)),
        in_specs=[vmem, vmem, vmem],
        out_specs=(
            pl.BlockSpec((PANEL, CHUNK), lambda i: (0, i)),
            pl.BlockSpec((PANEL, PANEL), lambda i: (0, 0)),
            pl.BlockSpec((PANEL, cols - PANEL), lambda i: (0, 0)),
            pl.BlockSpec((cols - PANEL, CHUNK), lambda i: (0, i))),
        scratch_shapes=[pltpu.VMEM((cols, 4 * PANEL), jnp.bfloat16)],
        compiler_params=pltpu.CompilerParams(
            dimension_semantics=("arbitrary",), vmem_limit_bytes=24 << 20),
        name="update",
    )(snap, stack, total)


def solution(mesh):
    return jax.shard_map(
        functools.partial(local, mesh.shape["rows"]),
        mesh=mesh,
        in_specs=(P("seg", "rows"),),
        out_specs=(P("seg", "rows"), P("seg", None), P("seg", None), P("seg", "rows")),
        check_vma=False,
    )
```

```python
import functools

import jax
import jax.numpy as jnp
from jax import lax
from jax.experimental import pallas as pl
from jax.experimental.pallas import tpu as pltpu
from jax.sharding import PartitionSpec as P

PANEL = 32
CHUNK = 1024
LANES = 128
BLOCK = 8
MESH = pl.DeviceIdType.MESH


def split(value):
    high = value.astype(jnp.bfloat16)
    return high, (value - high.astype(jnp.float32)).astype(jnp.bfloat16)


def reduce_kernel(chips, x_hbm, snap, stack, total, acc, part, pair_in, slots, full,
                  load_sem, pair_send, pair_recv, chip_send, chip_recv, last_send, last_recv):
    me = lax.axis_index("rows")
    core = lax.rem(me, 2)
    chip = lax.div(me, 2)
    partner = me + 1 - 2 * core
    cols, width = snap.shape
    chunks = width // CHUNK

    def load(c):
        where = pl.ds(pl.multiple_of(c * CHUNK, CHUNK), CHUNK)
        return pltpu.make_async_copy(x_hbm.at[:, where], snap.at[:, where], load_sem.at[c])

    for c in range(chunks):
        load(c).start()

    barrier = pltpu.get_barrier_semaphore()
    pl.semaphore_signal(barrier, inc=1, device_id={"rows": partner}, device_id_type=MESH)
    for k in range(1, chips):
        peer = lax.rem(chip + k, chips) * 2 + core
        pl.semaphore_signal(barrier, inc=1, device_id={"rows": peer}, device_id_type=MESH)

    acc[...] = jnp.zeros_like(acc)
    for c in range(chunks):
        load(c).wait()
        where = pl.ds(c * CHUNK, CHUNK)
        high, low = split(snap[:, where])
        panel = jnp.concatenate([high[:PANEL], low[:PANEL]], axis=0)
        stack[:, where] = panel
        acc[...] += lax.dot_general(
            jnp.concatenate([high, low], axis=0), panel, (((1,), (1,)), ((), ())),
            preferred_element_type=jnp.float32)
    both = acc[:cols] + acc[cols:]
    gram = (both[:, :PANEL] + both[:, PANEL:]).T
    half = PANEL // 2
    part[0] = gram[:half]
    part[1] = gram[half:]

    pl.semaphore_wait(barrier, chips)
    pair = pltpu.make_async_remote_copy(
        src_ref=part.at[1 - core], dst_ref=pair_in, send_sem=pair_send, recv_sem=pair_recv,
        device_id={"rows": partner}, device_id_type=MESH)
    pair.start()
    pair.wait()
    slots[chip] = part[core] + pair_in[...]

    def send(k):
        peer = lax.rem(chip + k, chips) * 2 + core
        return pltpu.make_async_remote_copy(
            src_ref=slots.at[chip], dst_ref=slots.at[chip], send_sem=chip_send.at[k - 1],
            recv_sem=chip_recv.at[k - 1], device_id={"rows": peer}, device_id_type=MESH)

    for k in range(1, chips):
        send(k).start()
    for k in range(1, chips):
        send(k).wait_recv()
    whole = slots[0]
    for k in range(1, chips):
        whole = whole + slots[k]
    full[core] = whole
    last = pltpu.make_async_remote_copy(
        src_ref=full.at[core], dst_ref=full.at[core], send_sem=last_send, recv_sem=last_recv,
        device_id={"rows": partner}, device_id_type=MESH)
    last.start()
    for k in range(1, chips):
        send(k).wait_send()
    last.wait()
    total[...] = full[...]


def eliminate(total, tiles):
    groups = PANEL // 8
    rows = lax.broadcasted_iota(jnp.int32, (8, LANES), 0)
    lanes = lax.broadcasted_iota(jnp.int32, (8, LANES), 1)
    a = [[total[8 * g:8 * g + 8, LANES * t:LANES * (t + 1)] for g in range(groups)] for t in range(tiles)]
    a.append([jnp.where(lanes == rows + 8 * g, 1.0, 0.0) for g in range(groups)])
    kept = [[None] * groups for _ in a]
    pivots = [None] * groups
    for start in range(0, PANEL, BLOCK):
        columns = [
            [jnp.broadcast_to(block[:, j:j + 1], (8, LANES)) for block in a[0]]
            for j in range(start, start + BLOCK)]
        for k in range(BLOCK):
            j = start + k
            group, at = j // 8, rows == j % 8
            column = columns[k]
            pivot = column[group][j % 8:j % 8 + 1]
            recip = 1.0 / pivot

            def step(blocks):
                row = blocks[group][j % 8:j % 8 + 1] * recip
                updated = [block - scale * row for block, scale in zip(blocks, column)]
                updated[group] = jnp.where(at, row, updated[group])
                return updated

            for t in range(len(a)):
                old = a[t][group]
                kept[t][group] = old if j % 8 == 0 else jnp.where(at, old, kept[t][group])
            pivots[group] = pivot if j % 8 == 0 else jnp.where(at, pivot, pivots[group])
            columns[k + 1:] = [step(blocks) for blocks in columns[k + 1:]]
            a = [step(blocks) for blocks in a]
    for g in range(groups):
        scale = 1.0 / jnp.sqrt(pivots[g])
        for t in range(len(a)):
            kept[t][g] = kept[t][g] * scale
        kept[0][g] = jnp.where((lanes >= rows + 8 * g) | (lanes >= PANEL), kept[0][g], 0.0)
        kept[tiles][g] = jnp.where(lanes <= rows + 8 * g, kept[tiles][g], 0.0)
    join = lambda blocks: jnp.concatenate(blocks, axis=0)
    solved = jnp.concatenate([join(a[t]) for t in range(tiles)], axis=1)
    upper = jnp.concatenate([join(kept[t]) for t in range(tiles)], axis=1)
    return upper, join(kept[tiles])[:, :PANEL], solved


def update_kernel(snap, stack, total, q_ref, r_ref, projected_ref, trailing_ref,
                  out, r_buf, projected_buf, sems):
    cols, width = snap.shape
    upper, lower, solved = eliminate(total[...].reshape(PANEL, cols), cols // LANES)
    r_buf[...] = upper[:, :PANEL]
    projected_buf[...] = upper[:, PANEL:]
    copies = [
        pltpu.make_async_copy(r_buf, r_ref, sems.at[0]),
        pltpu.make_async_copy(projected_buf, projected_ref, sems.at[1])]
    for copy in copies:
        copy.start()
    weights = jnp.concatenate([lower, -(solved.T)[PANEL:]], axis=0)
    high, low = split(weights)
    coef = jnp.concatenate([high, high, low, low], axis=1)
    for c in range(width // CHUNK):
        where = pl.ds(c * CHUNK, CHUNK)
        panel = stack[:, where]
        delta = lax.dot_general(
            coef, jnp.concatenate([panel, panel], axis=0), (((1,), (0,)), ((), ())),
            preferred_element_type=jnp.float32)
        out[:PANEL, where] = delta[:PANEL]
        out[PANEL:, where] = snap[PANEL:, where] + delta[PANEL:]
        for ref, rows, sem in ((q_ref, pl.ds(0, PANEL), 2 * c + 2), (trailing_ref, pl.ds(PANEL, cols - PANEL), 2 * c + 3)):
            copy = pltpu.make_async_copy(out.at[rows, where], ref.at[:, where], sems.at[sem])
            copy.start()
            copies.append(copy)
    for copy in copies:
        copy.wait()


def local(rows, snapshots):
    cols, width = snapshots.shape
    chips = rows // 2
    half = PANEL // 2
    f32 = jnp.float32
    vmem = pl.BlockSpec(memory_space=pltpu.VMEM)
    snap, stack, total = pl.pallas_call(
        functools.partial(reduce_kernel, chips),
        out_shape=(
            pltpu.VMEM((cols, width), f32),
            pltpu.VMEM((2 * PANEL, width), jnp.bfloat16),
            pltpu.VMEM((2, half, cols), f32)),
        in_specs=[pl.BlockSpec(memory_space=pltpu.HBM)],
        out_specs=(vmem, vmem, vmem),
        scratch_shapes=[
            pltpu.VMEM((2 * cols, 2 * PANEL), f32),
            pltpu.VMEM((2, half, cols), f32),
            pltpu.VMEM((half, cols), f32),
            pltpu.VMEM((chips, half, cols), f32),
            pltpu.VMEM((2, half, cols), f32),
            pltpu.SemaphoreType.DMA((width // CHUNK,)),
            pltpu.SemaphoreType.DMA,
            pltpu.SemaphoreType.DMA,
            pltpu.SemaphoreType.DMA((chips - 1,)),
            pltpu.SemaphoreType.DMA((chips - 1,)),
            pltpu.SemaphoreType.DMA,
            pltpu.SemaphoreType.DMA,
        ],
        compiler_params=pltpu.CompilerParams(
            collective_id=0, has_side_effects=True, vmem_limit_bytes=50 << 20),
        name="reduce",
    )(snapshots)
    return pl.pallas_call(
        update_kernel,
        out_shape=(
            jax.ShapeDtypeStruct((PANEL, width), f32),
            jax.ShapeDtypeStruct((PANEL, PANEL), f32),
            jax.ShapeDtypeStruct((PANEL, cols - PANEL), f32),
            jax.ShapeDtypeStruct((cols - PANEL, width), f32)),
        in_specs=[vmem, vmem, vmem],
        out_specs=(pl.BlockSpec(memory_space=pltpu.HBM),) * 4,
        scratch_shapes=[
            pltpu.VMEM((cols, width), f32),
            pltpu.VMEM((PANEL, PANEL), f32),
            pltpu.VMEM((PANEL, cols - PANEL), f32),
            pltpu.SemaphoreType.DMA((2 * (width // CHUNK) + 2,)),
        ],
        compiler_params=pltpu.CompilerParams(vmem_limit_bytes=32 << 20),
        name="update",
    )(snap, stack, total)


def solution(mesh):
    return jax.shard_map(
        functools.partial(local, mesh.shape["rows"]),
        mesh=mesh,
        in_specs=(P("seg", "rows"),),
        out_specs=(P("seg", "rows"), P("seg", None), P("seg", None), P("seg", "rows")),
        check_vma=False,
    )
```

```python
import functools

import jax
import jax.numpy as jnp
from jax import lax
from jax.experimental import pallas as pl
from jax.experimental.pallas import tpu as pltpu
from jax.sharding import PartitionSpec as P

PANEL = 32
LOADS = (2, 2, 2, 2)
STORES = (1, 1, 1, 1, 1, 1, 1, 1)
LANES = 128
BLOCK = 8
MESH = pl.DeviceIdType.MESH


def split(value):
    high = value.astype(jnp.bfloat16)
    return high, (value - high.astype(jnp.float32)).astype(jnp.bfloat16)


def spans(width, shares):
    ends = [width * sum(shares[:i]) // sum(shares) for i in range(len(shares) + 1)]
    return [pl.ds(low, high - low) for low, high in zip(ends, ends[1:])]


def reduce_kernel(chips, x_hbm, snap, stack, total, acc, part, pair_in, slots, full,
                  load_sem, pair_send, pair_recv, chip_send, chip_recv, last_send, last_recv):
    me = lax.axis_index("rows")
    core = lax.rem(me, 2)
    chip = lax.div(me, 2)
    partner = me + 1 - 2 * core
    cols, width = snap.shape
    loads = spans(width, LOADS)

    def load(c):
        return pltpu.make_async_copy(x_hbm.at[:, loads[c]], snap.at[:, loads[c]], load_sem.at[c])

    for c in range(len(loads)):
        load(c).start()

    barrier = pltpu.get_barrier_semaphore()
    pl.semaphore_signal(barrier, inc=1, device_id={"rows": partner}, device_id_type=MESH)
    for k in range(1, chips):
        peer = lax.rem(chip + k, chips) * 2 + core
        pl.semaphore_signal(barrier, inc=1, device_id={"rows": peer}, device_id_type=MESH)

    acc[...] = jnp.zeros_like(acc)
    for c in range(len(loads)):
        load(c).wait()
        where = loads[c]
        high, low = split(snap[:, where])
        panel = jnp.concatenate([high[:PANEL], low[:PANEL]], axis=0)
        stack[:, where] = panel
        acc[...] += lax.dot_general(
            high, panel, (((1,), (1,)), ((), ())), preferred_element_type=jnp.float32) + lax.dot_general(
            low, panel, (((1,), (1,)), ((), ())), preferred_element_type=jnp.float32)
    both = acc[...]
    gram = (both[:, :PANEL] + both[:, PANEL:]).T
    half = PANEL // 2
    part[0] = gram[:half]
    part[1] = gram[half:]

    pl.semaphore_wait(barrier, chips)
    pair = pltpu.make_async_remote_copy(
        src_ref=part.at[1 - core], dst_ref=pair_in, send_sem=pair_send, recv_sem=pair_recv,
        device_id={"rows": partner}, device_id_type=MESH)
    pair.start()
    pair.wait()
    slots[chip] = part[core] + pair_in[...]

    def send(k):
        peer = lax.rem(chip + k, chips) * 2 + core
        return pltpu.make_async_remote_copy(
            src_ref=slots.at[chip], dst_ref=slots.at[chip], send_sem=chip_send.at[k - 1],
            recv_sem=chip_recv.at[k - 1], device_id={"rows": peer}, device_id_type=MESH)

    for k in range(1, chips):
        send(k).start()
    for k in range(1, chips):
        send(k).wait_recv()
    whole = slots[0]
    for k in range(1, chips):
        whole = whole + slots[k]
    full[core] = whole
    last = pltpu.make_async_remote_copy(
        src_ref=full.at[core], dst_ref=full.at[core], send_sem=last_send, recv_sem=last_recv,
        device_id={"rows": partner}, device_id_type=MESH)
    last.start()
    for k in range(1, chips):
        send(k).wait_send()
    last.wait()
    total[...] = full[...]


def eliminate(total, tiles):
    groups = PANEL // 8
    rows = lax.broadcasted_iota(jnp.int32, (8, LANES), 0)
    lanes = lax.broadcasted_iota(jnp.int32, (8, LANES), 1)
    a = [[total[8 * g:8 * g + 8, LANES * t:LANES * (t + 1)] for g in range(groups)] for t in range(tiles)]
    a.append([jnp.where(lanes == rows + 8 * g, 1.0, 0.0) for g in range(groups)])
    kept = [[None] * groups for _ in a]
    pivots = [None] * groups
    for start in range(0, PANEL, BLOCK):
        columns = [
            [jnp.broadcast_to(block[:, j:j + 1], (8, LANES)) for block in a[0]]
            for j in range(start, start + BLOCK)]
        for k in range(BLOCK):
            j = start + k
            group, at = j // 8, rows == j % 8
            column = columns[k]
            pivot = column[group][j % 8:j % 8 + 1]
            recip = 1.0 / pivot

            def step(blocks):
                row = blocks[group][j % 8:j % 8 + 1] * recip
                updated = [block - scale * row for block, scale in zip(blocks, column)]
                updated[group] = jnp.where(at, row, updated[group])
                return updated

            for t in range(len(a)):
                old = a[t][group]
                kept[t][group] = old if j % 8 == 0 else jnp.where(at, old, kept[t][group])
            pivots[group] = pivot if j % 8 == 0 else jnp.where(at, pivot, pivots[group])
            columns[k + 1:] = [step(blocks) for blocks in columns[k + 1:]]
            a = [step(blocks) for blocks in a]
    for g in range(groups):
        scale = 1.0 / jnp.sqrt(pivots[g])
        for t in range(len(a)):
            kept[t][g] = kept[t][g] * scale
        kept[0][g] = jnp.where((lanes >= rows + 8 * g) | (lanes >= PANEL), kept[0][g], 0.0)
        kept[tiles][g] = jnp.where(lanes <= rows + 8 * g, kept[tiles][g], 0.0)
    join = lambda blocks: jnp.concatenate(blocks, axis=0)
    solved = jnp.concatenate([join(a[t]) for t in range(tiles)], axis=1)
    upper = jnp.concatenate([join(kept[t]) for t in range(tiles)], axis=1)
    return upper, join(kept[tiles])[:, :PANEL], solved


def update_kernel(snap, stack, total, q_ref, r_ref, projected_ref, trailing_ref,
                  out, r_buf, projected_buf, sems):
    cols, width = snap.shape
    upper, lower, solved = eliminate(total[...].reshape(PANEL, cols), cols // LANES)
    r_buf[...] = upper[:, :PANEL]
    projected_buf[...] = upper[:, PANEL:]
    copies = [
        pltpu.make_async_copy(r_buf, r_ref, sems.at[0]),
        pltpu.make_async_copy(projected_buf, projected_ref, sems.at[1])]
    for copy in copies:
        copy.start()
    weights = jnp.concatenate([lower, -(solved.T)[PANEL:]], axis=0)
    high, low = split(weights)
    coef = jnp.concatenate([high, high, low, low], axis=1)
    for c, where in enumerate(spans(width, STORES)):
        panel = stack[:, where]
        delta = lax.dot_general(
            coef, jnp.concatenate([panel, panel], axis=0), (((1,), (0,)), ((), ())),
            preferred_element_type=jnp.float32)
        out[:PANEL, where] = delta[:PANEL]
        out[PANEL:, where] = snap[PANEL:, where] + delta[PANEL:]
        for ref, rows, sem in ((q_ref, pl.ds(0, PANEL), 2 * c + 2), (trailing_ref, pl.ds(PANEL, cols - PANEL), 2 * c + 3)):
            copy = pltpu.make_async_copy(out.at[rows, where], ref.at[:, where], sems.at[sem])
            copy.start()
            copies.append(copy)
    for copy in copies:
        copy.wait()


def local(rows, snapshots):
    cols, width = snapshots.shape
    chips = rows // 2
    half = PANEL // 2
    f32 = jnp.float32
    vmem = pl.BlockSpec(memory_space=pltpu.VMEM)
    snap, stack, total = pl.pallas_call(
        functools.partial(reduce_kernel, chips),
        out_shape=(
            pltpu.VMEM((cols, width), f32),
            pltpu.VMEM((2 * PANEL, width), jnp.bfloat16),
            pltpu.VMEM((2, half, cols), f32)),
        in_specs=[pl.BlockSpec(memory_space=pltpu.HBM)],
        out_specs=(vmem, vmem, vmem),
        scratch_shapes=[
            pltpu.VMEM((cols, 2 * PANEL), f32),
            pltpu.VMEM((2, half, cols), f32),
            pltpu.VMEM((half, cols), f32),
            pltpu.VMEM((chips, half, cols), f32),
            pltpu.VMEM((2, half, cols), f32),
            pltpu.SemaphoreType.DMA((len(LOADS),)),
            pltpu.SemaphoreType.DMA,
            pltpu.SemaphoreType.DMA,
            pltpu.SemaphoreType.DMA((chips - 1,)),
            pltpu.SemaphoreType.DMA((chips - 1,)),
            pltpu.SemaphoreType.DMA,
            pltpu.SemaphoreType.DMA,
        ],
        compiler_params=pltpu.CompilerParams(
            collective_id=0, has_side_effects=True, vmem_limit_bytes=50 << 20),
        name="reduce",
    )(snapshots)
    return pl.pallas_call(
        update_kernel,
        out_shape=(
            jax.ShapeDtypeStruct((PANEL, width), f32),
            jax.ShapeDtypeStruct((PANEL, PANEL), f32),
            jax.ShapeDtypeStruct((PANEL, cols - PANEL), f32),
            jax.ShapeDtypeStruct((cols - PANEL, width), f32)),
        in_specs=[vmem, vmem, vmem],
        out_specs=(pl.BlockSpec(memory_space=pltpu.HBM),) * 4,
        scratch_shapes=[
            pltpu.VMEM((cols, width), f32),
            pltpu.VMEM((PANEL, PANEL), f32),
            pltpu.VMEM((PANEL, cols - PANEL), f32),
            pltpu.SemaphoreType.DMA((2 * len(STORES) + 2,)),
        ],
        compiler_params=pltpu.CompilerParams(vmem_limit_bytes=32 << 20),
        name="update",
    )(snap, stack, total)


def solution(mesh):
    return jax.shard_map(
        functools.partial(local, mesh.shape["rows"]),
        mesh=mesh,
        in_specs=(P("seg", "rows"),),
        out_specs=(P("seg", "rows"), P("seg", None), P("seg", None), P("seg", "rows")),
        check_vma=False,
    )
```
